32 devices in a mesh: band: 4 (over x, core), grid: 8 (over z, y).
Axes of the slice: x: 2, y: 2, z: 4, core: 2. Of those that a mesh axis runs over, the one named last changes fastest.
Arguments:
- orbitals: bfloat16 [16384, 2048], P('grid', 'band'), may hold values from -6 to 6
- projectors: bfloat16 [64, 8, 128], replicated, may hold values from -0.5 to 0.5
- sphere_start: int32 [64], replicated, may hold values from 0 to 1920, as said below
- proj_count: int32 [64], replicated, may hold values from 1 to 8
- owner_slab: int32 [64], replicated, may hold values from 0 to 7, as said below
- correlation_coef: float32 [64, 8, 8], replicated, as said below
Outputs:
- rotated: bfloat16 [16384, 2048], P(('grid', 'band'))
The draws below stay inside these ranges and needn't reach their ends.
Inputs may be any that keep to these rules, and one draw needn't show every extreme that they name: `sphere_start`: a multiple of 128. `owner_slab`: every slab owns exactly 8 atoms. `correlation_coef`: each atom's matrix is symmetric positive definite.
All inputs are finite; a program needn't handle non-finite values.
Results may differ from the reference program's by a relative error of at most 0.0049.
Values may be sent and summed in bfloat16 or wider, within the bound.
A program may use at most 128 MiB of HBM per device.

```python
import jax
import jax.numpy as jnp
from jax import lax

NB = 2048
SPH = 128
NPMAX = 8
A_SLAB = 8
G_SLAB = 2048
NG = 16384
NA = 64


def draw_owner_slab(key, part):
    order = jax.random.permutation(jax.random.fold_in(key, 11), NA)
    return (order // A_SLAB).astype(jnp.int32)


def draw_sphere_start(key, part):
    blocks = jax.random.randint(jax.random.fold_in(key, 12), (NA,), 0, G_SLAB // SPH)
    return (blocks * SPH).astype(jnp.int32)


def draw_correlation_coef(key, part):
    noise_key = jax.random.fold_in(key, 13)
    factor = jax.random.normal(noise_key, (NA, NPMAX, NPMAX), jnp.float32)
    square = jnp.einsum('aik,ajk->aij', factor, factor) / NPMAX
    square = square + 0.5 * jnp.eye(NPMAX, dtype=jnp.float32)[None, :, :]
    return (square / (NA * NPMAX)).astype(jnp.float32)


def touch_ends(values, stream_key, least, high):
    longest = values.shape.index(max(values.shape))
    spots = []
    for shift in (0, 1):
        where = [jax.random.randint(jax.random.fold_in(stream_key, axis), (), 0, length) for axis, length in enumerate(values.shape)]
        where[longest] = (where[longest] + shift) % values.shape[longest]
        spots.append(tuple(where))
    return values.at[spots[0]].set(least).at[spots[1]].set(high)


def shard_levels(stream_key, dims, pieces, low, high):
    loudness, own = 1.0, jax.random.fold_in(stream_key, 6)
    for position, blocks in pieces:
        heights = jnp.exp(jax.random.uniform(jax.random.fold_in(own, position), (blocks,), jnp.float32, low / len(pieces), high / len(pieces)))
        loudness = loudness * jnp.repeat(heights, dims[position] // blocks).reshape([-1 if axis == position else 1 for axis in range(len(dims))])
    return loudness


def centred(own_key, extent, width, bound, shards=(), kind=jnp.bfloat16):
    values = width * jax.random.normal(own_key, extent, jnp.float32)
    if shards:
        values = values * shard_levels(own_key, extent, shards, -0.22, 0.18)
    return jnp.clip(values, -bound, bound).astype(kind)


def setup_inputs(seed: int = 0) -> dict:
    key_of = jax.random.split(jax.random.key(seed), 7)
    orbitals = centred(key_of[0], (NG, NB), 1.0, 6.0, ((0, 8), (1, 4)))
    projectors = centred(key_of[1], (NA, NPMAX, SPH), SPH ** -0.5, 0.5)
    sphere_start = draw_sphere_start(jax.random.fold_in(key_of[6], 71), 0)
    proj_count = touch_ends(jax.random.randint(key_of[3], (NA,), 1, NPMAX + 1), jax.random.fold_in(key_of[3], 1), 1, NPMAX).astype(jnp.int32)
    owner_slab = draw_owner_slab(jax.random.fold_in(key_of[6], 71), 0)
    correlation_coef = draw_correlation_coef(jax.random.fold_in(key_of[6], 71), 0)
    return {"orbitals": orbitals, "projectors": projectors, "sphere_start": sphere_start, "proj_count": proj_count, "owner_slab": owner_slab, "correlation_coef": correlation_coef}


def inverse_factor(matrix):
    order = matrix.shape[0]
    if order <= 512 or order % 2 != 0:
        lower = jnp.linalg.cholesky(matrix)
        identity = jnp.eye(order, dtype=matrix.dtype)
        return lax.linalg.triangular_solve(lower, identity, left_side=True, lower=True)
    half = order // 2
    upper_inv = inverse_factor(matrix[:half, :half])
    below = jnp.dot(matrix[half:, :half], upper_inv.T, precision=lax.Precision.HIGHEST)
    schur = matrix[half:, half:] - jnp.dot(below, below.T, precision=lax.Precision.HIGHEST)
    lower_inv = inverse_factor(schur)
    corner = -jnp.dot(lower_inv, jnp.dot(below, upper_inv, precision=lax.Precision.HIGHEST), precision=lax.Precision.HIGHEST)
    top = jnp.concatenate([upper_inv, jnp.zeros((half, order - half), matrix.dtype)], axis=1)
    bottom = jnp.concatenate([corner, lower_inv], axis=1)
    return jnp.concatenate([top, bottom], axis=0)

def reference(orbitals, projectors, sphere_start, proj_count, owner_slab, correlation_coef):
    total_rows = orbitals.shape[0]
    bands = orbitals.shape[1]
    gram = jnp.dot(orbitals.T.astype(jnp.float32), orbitals.astype(jnp.float32), preferred_element_type=jnp.float32) * (1.0 / total_rows)
    starts = (owner_slab * G_SLAB + sphere_start).astype(jnp.int32)

    def one_atom(packed):
        weights, start, number, coefs = packed
        sphere_rows = lax.dynamic_slice_in_dim(orbitals, start, SPH, 0)
        correlations = jnp.dot(weights.astype(jnp.float32), sphere_rows.astype(jnp.float32), preferred_element_type=jnp.float32)
        active = jnp.arange(NPMAX) < number
        correlations = jnp.where(active[:, None], correlations, jnp.zeros_like(correlations))
        weighted = jnp.dot(coefs, correlations, precision=lax.Precision.HIGHEST)
        return (correlations, weighted)
    correlations, weighted = lax.map(one_atom, (projectors, starts, proj_count, correlation_coef))
    paw = jnp.dot(weighted.reshape(-1, bands).T, correlations.reshape(-1, bands), precision=lax.Precision.HIGHEST)
    metric = gram + paw
    inverse = inverse_factor(metric).astype(jnp.bfloat16)
    return jnp.dot(orbitals.astype(jnp.float32), inverse.T.astype(jnp.float32), preferred_element_type=jnp.float32).astype(jnp.bfloat16)
```

```python
import jax
import jax.numpy as jnp
from jax import lax
from jax.experimental import pallas as pl
from jax.experimental.pallas import tpu as pltpu
from jax.sharding import PartitionSpec as P

SPH = 128
NPMAX = 8
A_SLAB = 8
BLK = 256
TOL = 4e-6
STEPS = 10


def bdot(a, b, dims):
    return lax.dot_general(
        a.astype(jnp.bfloat16), b.astype(jnp.bfloat16), (dims, ((), ())),
        preferred_element_type=jnp.float32,
    )


def split_bf16(a):
    high = a.astype(jnp.bfloat16)
    return high, (a - high.astype(jnp.float32)).astype(jnp.bfloat16)


def bdot3(a, b, dims):
    ah, al = split_bf16(a)
    bh, bl = split_bf16(b)
    return bdot(ah, bh, dims) + (bdot(ah, bl, dims) + bdot(al, bh, dims))


def block_inverse(a, w_ref):
    rows = lax.broadcasted_iota(jnp.int32, a.shape, 0)
    cols = lax.broadcasted_iota(jnp.int32, a.shape, 1)
    diag = rows == cols
    phi_mask = jnp.where(rows > cols, 1.0, jnp.where(diag, 0.5, 0.0))
    on_diag = jnp.where(diag, a, 0.0)
    scale_col = lax.rsqrt(jnp.sum(on_diag, axis=1, keepdims=True))
    scale_row = lax.rsqrt(jnp.sum(on_diag, axis=0, keepdims=True))
    e0 = jnp.where(diag, 0.0, a * scale_col * scale_row)

    def residual(v, dot=bdot):
        t = dot(v, e0, ((1,), (0,)))
        return (
            e0 + v + jnp.where(diag, v, 0.0) + t + dot(e0 + v + t, v, ((1,), (1,)))
        ) * phi_mask

    def step(carry):
        v, phi, _, count = carry
        v = v - phi - bdot(phi, v, ((1,), (0,)))
        phi = residual(v)
        return v, phi, jnp.sum(phi * phi), count + 1

    v = -e0 * phi_mask
    phi = residual(v)
    start = (v, phi, jnp.sum(phi * phi), jnp.int32(0))
    v, phi, err, _ = lax.while_loop(
        lambda c: jnp.logical_and(jnp.logical_not(c[2] < TOL), c[3] < STEPS), step, start
    )
    v = v - phi
    phi = residual(v, bdot3)
    v = v - phi - bdot(phi, v, ((1,), (0,)))
    w_ref[...] = (v + jnp.where(diag, 1.0, 0.0)) * scale_row

    @pl.when(jnp.logical_not(err < TOL))
    def _():
        w_ref[...] = jnp.where(rows <= cols, a, 0.0)

        def column(j, _):
            b = w_ref[...]
            line = jnp.sum(jnp.where(rows == j, b, 0.0), axis=0, keepdims=True)
            lane = lax.broadcasted_iota(jnp.int32, line.shape, 1)
            pivot = jnp.sum(jnp.where(lane == j, line, 0.0), axis=1, keepdims=True)
            q = jnp.where(lane == j, 1.0, line) * lax.rsqrt(pivot)
            spread = jnp.broadcast_to(q, b.shape)
            factor = jnp.sum(jnp.where(diag, spread, 0.0), axis=1, keepdims=True)
            keep = (cols <= j) | (cols >= rows)
            below = b - jnp.where(keep, factor * q, 0.0)
            w_ref[...] = jnp.where(rows == j, q, jnp.where(rows > j, below, b))
            return 0

        lax.fori_loop(0, a.shape[0], column, 0)
        w_ref[...] = jnp.where(rows >= cols, w_ref[...], 0.0)


def factor_kernel(packed_ref, out_ref, work, wblk, q):
    n = out_ref.shape[0]
    blocks = n // BLK
    for i in range(blocks // 2):
        band = slice(i * BLK, (i + 1) * BLK)
        j = blocks - 1 - i
        cut = n - i * BLK
        for row, lo, hi in ((i, 0, cut), (j, cut, n + BLK)):
            rows = slice(row * BLK, (row + 1) * BLK)
            if row:
                work[rows, : row * BLK] = jnp.zeros((BLK, row * BLK), jnp.float32)
            work[rows, row * BLK :] = packed_ref[band, lo:hi].astype(jnp.float32)

    def at(i):
        return pl.ds(pl.multiple_of(i * BLK, BLK), BLK)

    def pivot(k, _):
        block_inverse(work[at(k), at(k)], wblk)
        w = wblk[...]

        def line(j, _):
            q[:, at(j)] = bdot3(w, work[at(k), at(j)], ((1,), (0,))).astype(jnp.bfloat16)
            return 0

        lax.fori_loop(0, blocks, line, 0)
        q[:, at(k)] = w.astype(jnp.bfloat16)

        def store(j, _):
            out_ref[at(k), at(j)] = q[:, at(j)]
            return 0

        def clear(j, _):
            out_ref[at(k), at(j)] = jnp.zeros((BLK, BLK), jnp.bfloat16)
            return 0

        lax.fori_loop(0, k + 1, store, 0)
        lax.fori_loop(k + 1, blocks, clear, 0)

        def below(i, _):
            p = q[:, at(i)].T

            def update(j, _):
                work[at(i), at(j)] -= bdot(p, q[:, at(j)], ((1,), (0,)))
                return 0

            lax.fori_loop(0, k + 1, update, 0)
            lax.fori_loop(i, blocks, update, 0)
            return 0

        lax.fori_loop(k + 1, blocks, below, 0)
        return 0

    lax.fori_loop(0, blocks, pivot, 0)


def inverse_of_packed(packed, n):
    return pl.pallas_call(
        factor_kernel,
        out_shape=jax.ShapeDtypeStruct((n, n), jnp.bfloat16),
        in_specs=[pl.BlockSpec(memory_space=pltpu.VMEM)],
        out_specs=pl.BlockSpec(memory_space=pltpu.VMEM),
        scratch_shapes=[
            pltpu.VMEM((n, n), jnp.float32),
            pltpu.VMEM((BLK, BLK), jnp.float32),
            pltpu.VMEM((BLK, n), jnp.bfloat16),
        ],
        compiler_params=pltpu.CompilerParams(vmem_limit_bytes=56 * 1024 * 1024),
        name="inverse_factor",
    )(packed)


def slab_atoms(owner_slab, slab):
    mine = owner_slab == slab
    place = jnp.cumsum(mine.astype(jnp.int32)) - 1
    atoms = jnp.arange(owner_slab.shape[0], dtype=jnp.int32)
    hit = mine[None, :] & (place[None, :] == jnp.arange(A_SLAB, dtype=jnp.int32)[:, None])
    return jnp.sum(jnp.where(hit, atoms[None, :], 0), axis=1)


def atom_terms(source, weights, starts, counts, coefs):
    height = source.shape[0]
    atoms = weights.shape[0]
    active = jnp.arange(NPMAX)[None, :] < counts[:, None]
    here = jnp.arange(height // SPH)[None, :] * SPH == starts[:, None]
    keep = active[:, :, None, None] & here[:, None, :, None]
    spread = jnp.where(keep, weights[:, :, None, :], jnp.zeros((), weights.dtype))
    correlations = jnp.dot(
        spread.reshape(atoms * NPMAX, height), source, preferred_element_type=jnp.float32
    )
    same = jnp.eye(atoms, dtype=coefs.dtype)
    mixing = (same[:, None, :, None] * coefs[:, :, None, :]).reshape(atoms * NPMAX, -1)
    weighted = jnp.dot(mixing, correlations, precision=lax.Precision.HIGHEST)
    return (correlations, weighted)


def split_terms(x):
    high = lax.reduce_precision(x, 8, 7)
    return high.astype(jnp.bfloat16), (x - high).astype(jnp.bfloat16)


def shards(orbitals, projectors, sphere_start, proj_count, owner_slab, correlation_coef):
    band_index = lax.axis_index("band")
    slab = lax.axis_index("grid")
    total_rows = orbitals.shape[0] * lax.axis_size("grid")
    chosen = slab_atoms(owner_slab, slab)
    weights = projectors[chosen]
    counts = proj_count[chosen]
    coefs = correlation_coef[chosen]
    mine = lax.all_to_all(orbitals, "band", split_axis=0, concat_axis=1, tiled=True)
    height, width_all = mine.shape
    offsets = sphere_start[chosen] - band_index * height
    correlations, weighted = atom_terms(mine, weights, offsets, counts, coefs)
    wh, wl = split_terms(weighted * total_rows)
    ch, cl = split_terms(correlations)
    left = jnp.concatenate([mine, wh, wh, wl], axis=0)
    right = jnp.concatenate([mine, ch, cl, ch], axis=0)
    blocks = width_all // BLK

    def strip(i):
        rows = left[:, i * BLK : (i + 1) * BLK]
        return lax.dot_general(
            rows, right[:, i * BLK :], (((0,), (0,)), ((), ())),
            preferred_element_type=jnp.float32,
        ) * (1.0 / total_rows)

    packed = jnp.concatenate(
        [
            jnp.concatenate([strip(i), strip(blocks - 1 - i)], axis=1)
            for i in range(blocks // 2)
        ],
        axis=0,
    )
    part = lax.psum_scatter(packed, ("grid", "band"), scatter_dimension=0, tiled=True)
    whole = lax.all_gather(part, ("grid", "band"), axis=0, tiled=True)
    inverse = inverse_of_packed(whole, width_all)
    return lax.dot_general(
        mine, inverse, (((1,), (1,)), ((), ())), preferred_element_type=jnp.float32
    ).astype(jnp.bfloat16)


def solution(mesh):
    in_specs = (P("grid", "band"), P(), P(), P(), P(), P())
    out_specs = P(("grid", "band"), None)
    return jax.shard_map(shards, mesh=mesh, in_specs=in_specs, out_specs=out_specs, check_vma=False)
```
